32 devices in a mesh: band: 2 (over y), coarse: 4 (over x, core), fine: 4 (over z).
Axes of the slice: x: 2, y: 2, z: 4, core: 2. Of those that a mesh axis runs over, the one named last changes fastest.
Arguments:
- spectra: float32 [32, 8, 8192], P(None, ('band', 'coarse'), 'fine'), parts along dimension 1, may hold values from 0.2 to 5
Outputs:
- drift_power: float32 [8, 32, 8, 8192], P(None, None, ('band', 'coarse'), 'fine'), parts along dimension 2
The draws below stay inside these ranges and needn't reach their ends.
There are 2 independent parts, one for each index of `band`. The reference program is written for one: setup_inputs(seed, part) draws one part's arguments, and reference() takes and returns one part's arrays. A program takes and returns all parts, laid end to end along the dimension named above; each array names one. Nothing has to cross between parts.
All inputs are finite; a program needn't handle non-finite values.
Results may differ from the reference program's by a relative error of at most 0.00002.
Values sent between devices are 32-bit elements; how exact they have to be, the bound alone decides.
A program may use at most 64 MiB of HBM per device.

```python
import math
import jax
import jax.numpy as jnp

ROWS = 32
RATES = 8
FINE = 8192
COARSE = 4


def levels(own_key, dims, split, least, top_value):
    gain, own = 1.0, jax.random.fold_in(own_key, 6)
    for axis_at, parts in split:
        draws = jnp.exp(jax.random.uniform(jax.random.fold_in(own, axis_at), (parts,), jnp.float32, least / len(split), top_value / len(split)))
        gain = gain * jnp.repeat(draws, dims[axis_at] // parts).reshape([-1 if axis == axis_at else 1 for axis in range(len(dims))])
    return gain


def setup_inputs(seed: int = 0, part: int = 0) -> dict:
    seeds = jax.random.split(jax.random.key(seed), 2)
    own_keys = jax.random.split(jax.random.fold_in(seeds[1], part), 2)
    return {
        "spectra": jnp.clip(jnp.exp(math.log(5.0) - 3.218876 * jax.random.uniform(own_keys[0], (ROWS, COARSE, FINE), jnp.float32) ** levels(own_keys[0], (ROWS, COARSE, FINE), ((1, 4), (2, 4)), -0.2, 0.2)), 0.2, 5.0),
    }


def shift_left(values, amount):
    if amount == 0:
        return values
    filler = jnp.zeros(values.shape[:-1] + (amount,), values.dtype)
    return jnp.concatenate([values[..., amount:], filler], axis=-1)


def drift_tree(rows_in):
    blocks = rows_in[:, None, :]
    stride = 1
    while stride < rows_in.shape[0]:
        firsts = blocks[0::2]
        seconds = blocks[1::2]
        even_part = jnp.stack([shift_left(seconds[:, position], position) for position in range(stride)], axis=1)
        odd_part = jnp.stack([shift_left(seconds[:, position], position + 1) for position in range(stride)], axis=1)
        joined = jnp.stack([firsts + even_part, firsts + odd_part], axis=2)
        blocks = joined.reshape(firsts.shape[0], 2 * stride, rows_in.shape[1])
        stride = stride * 2
    return blocks[0]


def reference(spectra):
    bandpass = jnp.sum(spectra, axis=1) / COARSE
    inverse = 1.0 / bandpass
    columns = COARSE * FINE
    normed = (spectra * inverse[:, None, :] - 1.0).reshape(ROWS, columns)
    margin = 4 * ROWS
    padded = jnp.pad(normed, ((0, 0), (margin, margin)))
    outputs = []
    for rate_index in range(RATES):
        row_slope = rate_index - RATES // 2
        sheared = jnp.stack([padded[row_index, margin + row_slope * row_index: margin + row_slope * row_index + columns] for row_index in range(ROWS)])
        outputs.append(drift_tree(sheared))
    return jnp.stack(outputs).reshape(RATES, ROWS, COARSE, FINE)
```

```python
import functools

import jax
import jax.numpy as jnp
from jax import lax
from jax.experimental import pallas as pl
from jax.experimental.pallas import tpu as pltpu
from jax.sharding import PartitionSpec as P

RATES = 8
LANES = 128
PIECES = 4
UNROLL = 2
ROW = 18
HEAD = 1
MESH = pl.DeviceIdType.MESH


def comm_kernel(
    channels, fines, rows, chunks, x_ref, e_ref,
    edge, hraw, part_a, sum_1, part_b, inv_1, part_c, halo_a, halo_1, halo_b, halo_i, halo_c,
    edge_send, edge_recv, a_send, a_recv, b_send, b_recv, c_send, c_recv,
):
    half_rows = rows // 2
    piece_rows = half_rows // PIECES
    size = piece_rows * chunks
    others = channels // 2 - 1
    c = lax.axis_index("coarse")
    f = lax.axis_index("fine")
    mine = c % 2
    pair = c // 2
    partner = {"coarse": pair * 2 + 1 - mine}
    peers = [{"coarse": ((pair + o) % (channels // 2)) * 2 + mine} for o in range(1, others + 1)]
    place = c * fines + f
    after = (place + 1) % (channels * fines)
    before = (place + channels * fines - 1) % (channels * fines)
    after_id = {"coarse": after // fines, "fine": after % fines}
    before_id = {"coarse": before // fines, "fine": before % fines}

    barrier = pltpu.get_barrier_semaphore()
    greet = [partner] + peers + [after_id, before_id]
    for device in greet:
        pl.semaphore_signal(barrier, inc=1, device_id=device, device_id_type=MESH)
    for half in range(2):
        start = half * half_rows * chunks
        edge[0, half] = x_ref[pl.ds(start + chunks - 1, half_rows, stride=chunks), :]
        edge[1, half] = x_ref[pl.ds(start, half_rows, stride=chunks), :]
    pl.semaphore_wait(barrier, len(greet))

    started = []

    def send(src, dst, send_sem, recv_sem, device):
        copy = pltpu.make_async_remote_copy(
            src_ref=src, dst_ref=dst, send_sem=send_sem, recv_sem=recv_sem,
            device_id=device, device_id_type=MESH,
        )
        copy.start()
        started.append(copy)
        return copy

    def piece_start(half, p):
        return pl.multiple_of((half * half_rows + p * piece_rows) * chunks, 8)

    halos = [
        send(edge.at[0], hraw.at[0], edge_send.at[0], edge_recv.at[0], after_id),
        send(edge.at[1], hraw.at[1], edge_send.at[1], edge_recv.at[1], before_id),
    ]
    theirs = 1 - mine
    a_copies = [
        send(x_ref.at[pl.ds(piece_start(theirs, p), size), :], part_a.at[p], a_send.at[p], a_recv.at[p], partner)
        for p in range(PIECES)
    ]
    b_copies = []
    for p in range(PIECES):
        a_copies[p].wait_recv()
        sum_1[p] = x_ref[pl.ds(piece_start(mine, p), size), :] + part_a[p]
        b_copies.append([
            send(sum_1.at[p], part_b.at[o, p], b_send.at[o, p], b_recv.at[o, p], peers[o])
            for o in range(others)
        ])
    for copy in halos:
        copy.wait_recv()
    halo_pair = [
        send(hraw.at[side, theirs], halo_a.at[side], a_send.at[PIECES + side], a_recv.at[PIECES + side], partner)
        for side in range(2)
    ]
    for side in range(2):
        halo_pair[side].wait_recv()
        halo_1[side] = hraw[side, mine] + halo_a[side]
    halo_b_copies = [
        send(halo_1, halo_b.at[o], b_send.at[o, PIECES], b_recv.at[o, PIECES], peers[o])
        for o in range(others)
    ]

    def put(half, p, inverse):
        normed = x_ref[pl.ds(piece_start(half, p), size), :] * inverse - 1.0
        for i in range(piece_rows):
            t = half * half_rows + p * piece_rows + i
            e_ref[pl.ds(t * ROW + HEAD, chunks), :] = normed[i * chunks : (i + 1) * chunks]

    c_copies = []
    for p in range(PIECES):
        total = sum_1[p]
        for o in range(others):
            b_copies[p][o].wait_recv()
            total = total + part_b[o, p]
        inv_1[p] = 1.0 / (total / channels)
        c_copies.append(send(inv_1.at[p], part_c.at[p], c_send.at[p], c_recv.at[p], partner))
        put(mine, p, inv_1[p])
    total = halo_1[...]
    for o in range(others):
        halo_b_copies[o].wait_recv()
        total = total + halo_b[o]
    halo_i[...] = 1.0 / (total / channels)
    halo_c_copy = send(halo_i, halo_c, c_send.at[PIECES], c_recv.at[PIECES], partner)

    at_edge = [place == 0, place == channels * fines - 1]
    at_row = [HEAD - 1, HEAD + chunks]

    def put_halo(half, inverse):
        for side in range(2):
            normed = hraw[side, half] * inverse[side] - 1.0
            normed = jnp.where(at_edge[side], jnp.zeros_like(normed), normed)
            for i in range(half_rows):
                t = half * half_rows + i
                e_ref[pl.ds(t * ROW + at_row[side], 1), :] = normed[i : i + 1]

    put_halo(mine, halo_i)
    for p in range(PIECES):
        c_copies[p].wait_recv()
        put(theirs, p, part_c[p])
    halo_c_copy.wait_recv()
    put_halo(theirs, halo_c)
    for copy in started:
        copy.wait_send()


def tree_kernel(channels, fines, rows, chunks, e_ref, out_hbm, out, halo, *rest):
    levels = (None,) + rest[:-1]
    out_sem = rest[-1]
    depth = len(levels)
    last = jnp.logical_and(
        lax.axis_index("coarse") == channels - 1, lax.axis_index("fine") == fines - 1
    )
    lane = lax.broadcasted_iota(jnp.int32, (chunks, LANES), 1)
    chunk = lax.broadcasted_iota(jnp.int32, (chunks, LANES), 0)
    final = chunk == chunks - 1
    edge = jnp.logical_and(jnp.logical_and(final, lane == LANES - 1), last)
    lane_q = lax.broadcasted_iota(jnp.int32, (RATES, LANES), 1)
    slope_q = RATES - 1 - RATES // 2 - lax.broadcasted_iota(jnp.int32, (RATES, LANES), 0)

    def at(q, row):
        return (q * rows + row) * chunks

    def left(value, amount):
        return value if amount % LANES == 0 else pltpu.roll(value, -amount % LANES, 1)

    for t in range(rows):
        base = t * ROW + HEAD + chunks
        inner = jnp.broadcast_to(e_ref[pl.ds(base - 1, 1), :], (RATES, LANES))
        outer = jnp.broadcast_to(e_ref[pl.ds(base, 1), :], (RATES, LANES))
        value = jnp.where(lane_q >= slope_q * t + LANES, inner, outer)
        value = left(value, (RATES - 1 - RATES // 2) * t)
        for part in (t // 2, t - t // 2):
            if part:
                value = pltpu.roll(value, 0, 1, stride=part, stride_axis=0)
        halo[0, t] = jnp.where(last, jnp.zeros_like(value), value)
    for level in range(depth - 1):
        m = 1 << level
        for r in range(rows // (2 * m)):
            for d in range(m):
                first = halo[level, 2 * r * m + d]
                second = halo[level, (2 * r + 1) * m + d]
                for odd in range(2):
                    halo[level + 1, r * 2 * m + 2 * d + odd] = first + left(second, d + odd)

    def windows(t):
        return [e_ref[pl.ds(t * ROW + HEAD + shift, chunks), :] for shift in (-1, 0, 1)]

    def shifted(seen, amount):
        down = 1 if amount >= 0 else 0
        lanes = amount % LANES
        if lanes == 0:
            return seen[down + (amount - lanes) // LANES + 1 - down]
        return left(jnp.where(lane >= lanes, seen[down], seen[down + 1]), lanes)

    for r in range(rows // 2):
        even, odd_row = windows(2 * r), windows(2 * r + 1)
        for q in range(RATES):
            slope = q - RATES // 2
            first = shifted(even, slope * 2 * r)
            second = shifted(odd_row, slope * (2 * r + 1))
            ahead = shifted(odd_row, slope * (2 * r + 1) + 1)
            ahead = jnp.where(edge, jnp.zeros_like(ahead), ahead)
            levels[1][pl.ds(at(q, 2 * r), chunks), :] = first + second
            levels[1][pl.ds(at(q, 2 * r + 1), chunks), :] = first + ahead

    def tree(step, carry):
        for level in range(1, depth):
            m = 1 << level
            source = levels[level]
            for r in range(rows // (2 * m)):
                for d in range(m):
                    for sub in range(UNROLL):
                        q = step * UNROLL + sub
                        row_b = (2 * r + 1) * m + d
                        where_b = pl.multiple_of(at(q, row_b), 8)
                        first = source[pl.ds(pl.multiple_of(at(q, 2 * r * m + d), 8), chunks), :]
                        second = source[pl.ds(where_b, chunks), :]
                        ahead = source[pl.ds(where_b + 1, chunks), :]
                        beyond = jnp.broadcast_to(halo[level, row_b, pl.ds(RATES - 1 - q, 1), :], (chunks, LANES))
                        ahead = jnp.where(final, beyond, ahead)
                        for odd in range(2):
                            k = d + odd
                            moved = second
                            if k:
                                moved = left(jnp.where(lane >= k, second, ahead), k)
                            row = r * 2 * m + 2 * d + odd
                            value = first + moved
                            if level + 1 < depth:
                                levels[level + 1][pl.ds(pl.multiple_of(at(q, row), 8), chunks), :] = value
                            else:
                                out[q, row * chunks : (row + 1) * chunks] = value
        for sub in range(UNROLL):
            q = step * UNROLL + sub
            pltpu.make_async_copy(out.at[q], out_hbm.at[q], out_sem.at[q]).start()
        return carry

    lax.fori_loop(0, RATES // UNROLL, tree, 0)
    for q in range(RATES):
        pltpu.make_async_copy(out.at[q], out_hbm.at[q], out_sem.at[q]).wait()


def on_device(channels, fines, spectra):
    rows, _, columns = spectra.shape
    chunks = columns // LANES
    depth = rows.bit_length() - 1
    assert (RATES // 2) * (rows - 1) <= LANES and rows == 1 << depth
    others = channels // 2 - 1
    half = rows // 2
    size = half // PIECES * chunks
    vmem = functools.partial(pltpu.VMEM, dtype=jnp.float32)
    dma = pltpu.SemaphoreType.DMA
    x = spectra.reshape(rows * chunks, LANES)
    normed = pl.pallas_call(
        functools.partial(comm_kernel, channels, fines, rows, chunks),
        out_shape=jax.ShapeDtypeStruct((rows * ROW, LANES), jnp.float32),
        in_specs=[pl.BlockSpec(memory_space=pltpu.VMEM)],
        out_specs=pl.BlockSpec(memory_space=pltpu.VMEM),
        scratch_shapes=[
            vmem((2, 2, half, LANES)), vmem((2, 2, half, LANES)),
            vmem((PIECES, size, LANES)), vmem((PIECES, size, LANES)),
            vmem((others, PIECES, size, LANES)), vmem((PIECES, size, LANES)), vmem((PIECES, size, LANES)),
            vmem((2, half, LANES)), vmem((2, half, LANES)), vmem((others, 2, half, LANES)),
            vmem((2, half, LANES)), vmem((2, half, LANES)),
            dma((2,)), dma((2,)), dma((PIECES + 2,)), dma((PIECES + 2,)),
            dma((others, PIECES + 1)), dma((others, PIECES + 1)), dma((PIECES + 1,)), dma((PIECES + 1,)),
        ],
        compiler_params=pltpu.CompilerParams(collective_id=0, has_side_effects=True),
        name="normalize",
    )(x)
    stored = RATES * rows * chunks + 8
    out = pl.pallas_call(
        functools.partial(tree_kernel, channels, fines, rows, chunks),
        out_shape=jax.ShapeDtypeStruct((RATES, rows * chunks, LANES), jnp.float32),
        in_specs=[pl.BlockSpec(memory_space=pltpu.VMEM)],
        out_specs=pl.BlockSpec(memory_space=pl.ANY),
        scratch_shapes=[vmem((RATES, rows * chunks, LANES)), vmem((depth, rows, RATES, LANES))]
        + [vmem((stored, LANES))] * (depth - 1)
        + [dma((RATES,))],
        compiler_params=pltpu.CompilerParams(vmem_limit_bytes=48 << 20),
        name="tree",
    )(normed)
    return out.reshape(RATES, rows, 1, columns)


def solution(mesh):
    body = functools.partial(on_device, mesh.shape["coarse"], mesh.shape["fine"])
    in_specs = (P(None, ("band", "coarse"), "fine"),)
    out_specs = P(None, None, ("band", "coarse"), "fine")
    return jax.shard_map(body, mesh=mesh, in_specs=in_specs, out_specs=out_specs, check_vma=False)
```

```python
import functools

import jax
import jax.numpy as jnp
from jax import lax
from jax.experimental import pallas as pl
from jax.experimental.pallas import tpu as pltpu
from jax.sharding import PartitionSpec as P

RATES = 8
LANES = 128
PIECES = 4
UNROLL = 2
ROW = 18
HEAD = 1
MESH = pl.DeviceIdType.MESH


def comm_kernel(
    channels, fines, rows, chunks, x_ref, e_ref,
    edge, hraw, part_a, sum_1, part_b, inv_1, part_c, halo_a, halo_1, halo_b, halo_i, halo_c,
    edge_send, edge_recv, a_send, a_recv, b_send, b_recv, c_send, c_recv,
):
    half_rows = rows // 2
    piece_rows = half_rows // PIECES
    size = piece_rows * chunks
    others = channels // 2 - 1
    c = lax.axis_index("coarse")
    f = lax.axis_index("fine")
    mine = c % 2
    pair = c // 2
    partner = {"coarse": pair * 2 + 1 - mine}
    peers = [{"coarse": ((pair + o) % (channels // 2)) * 2 + mine} for o in range(1, others + 1)]
    place = c * fines + f
    after = (place + 1) % (channels * fines)
    before = (place + channels * fines - 1) % (channels * fines)
    after_id = {"coarse": after // fines, "fine": after % fines}
    before_id = {"coarse": before // fines, "fine": before % fines}

    barrier = pltpu.get_barrier_semaphore()
    greet = [partner] + peers + [after_id, before_id]
    for device in greet:
        pl.semaphore_signal(barrier, inc=1, device_id=device, device_id_type=MESH)
    for half in range(2):
        start = half * half_rows * chunks
        edge[0, half] = x_ref[pl.ds(start + chunks - 1, half_rows, stride=chunks), :]
        edge[1, half] = x_ref[pl.ds(start, half_rows, stride=chunks), :]
    pl.semaphore_wait(barrier, len(greet))

    started = []

    def send(src, dst, send_sem, recv_sem, device):
        copy = pltpu.make_async_remote_copy(
            src_ref=src, dst_ref=dst, send_sem=send_sem, recv_sem=recv_sem,
            device_id=device, device_id_type=MESH,
        )
        copy.start()
        started.append(copy)
        return copy

    def piece_start(half, p):
        return pl.multiple_of((half * half_rows + p * piece_rows) * chunks, 8)

    halos = [
        send(edge.at[0], hraw.at[0], edge_send.at[0], edge_recv.at[0], after_id),
        send(edge.at[1], hraw.at[1], edge_send.at[1], edge_recv.at[1], before_id),
    ]
    theirs = 1 - mine
    a_copies = [
        send(x_ref.at[pl.ds(piece_start(theirs, p), size), :], part_a.at[p], a_send.at[p], a_recv.at[p], partner)
        for p in range(PIECES)
    ]
    b_copies = []
    for p in range(PIECES):
        a_copies[p].wait_recv()
        sum_1[p] = x_ref[pl.ds(piece_start(mine, p), size), :] + part_a[p]
        b_copies.append([
            send(sum_1.at[p], part_b.at[o, p], b_send.at[o, p], b_recv.at[o, p], peers[o])
            for o in range(others)
        ])
    for copy in halos:
        copy.wait_recv()
    halo_pair = [
        send(hraw.at[side, theirs], halo_a.at[side], a_send.at[PIECES + side], a_recv.at[PIECES + side], partner)
        for side in range(2)
    ]
    for side in range(2):
        halo_pair[side].wait_recv()
        halo_1[side] = hraw[side, mine] + halo_a[side]
    halo_b_copies = [
        send(halo_1, halo_b.at[o], b_send.at[o, PIECES], b_recv.at[o, PIECES], peers[o])
        for o in range(others)
    ]

    def put(half, p, inverse):
        normed = x_ref[pl.ds(piece_start(half, p), size), :] * inverse - 1.0
        for i in range(piece_rows):
            t = half * half_rows + p * piece_rows + i
            e_ref[pl.ds(t * ROW + HEAD, chunks), :] = normed[i * chunks : (i + 1) * chunks]

    c_copies = []
    for p in range(PIECES):
        total = sum_1[p]
        for o in range(others):
            b_copies[p][o].wait_recv()
            total = total + part_b[o, p]
        inv_1[p] = 1.0 / (total / channels)
        c_copies.append(send(inv_1.at[p], part_c.at[p], c_send.at[p], c_recv.at[p], partner))
        put(mine, p, inv_1[p])
    total = halo_1[...]
    for o in range(others):
        halo_b_copies[o].wait_recv()
        total = total + halo_b[o]
    halo_i[...] = 1.0 / (total / channels)
    halo_c_copy = send(halo_i, halo_c, c_send.at[PIECES], c_recv.at[PIECES], partner)

    at_edge = [place == 0, place == channels * fines - 1]
    at_row = [HEAD - 1, HEAD + chunks]

    def put_halo(half, inverse):
        for side in range(2):
            normed = hraw[side, half] * inverse[side] - 1.0
            normed = jnp.where(at_edge[side], jnp.zeros_like(normed), normed)
            for i in range(half_rows):
                t = half * half_rows + i
                e_ref[pl.ds(t * ROW + at_row[side], 1), :] = normed[i : i + 1]

    put_halo(mine, halo_i)
    for p in range(PIECES):
        c_copies[p].wait_recv()
        put(theirs, p, part_c[p])
    halo_c_copy.wait_recv()
    put_halo(theirs, halo_c)
    for copy in started:
        copy.wait_send()


def tree_kernel(channels, fines, rows, chunks, e_ref, out_hbm, out, halo, *rest):
    levels = (None,) + rest[:-1]
    out_sem = rest[-1]
    depth = len(levels)
    last = jnp.logical_and(
        lax.axis_index("coarse") == channels - 1, lax.axis_index("fine") == fines - 1
    )
    lane = lax.broadcasted_iota(jnp.int32, (chunks, LANES), 1)
    chunk = lax.broadcasted_iota(jnp.int32, (chunks, LANES), 0)
    final = chunk == chunks - 1
    edge = jnp.logical_and(jnp.logical_and(final, lane == LANES - 1), last)
    lane_q = lax.broadcasted_iota(jnp.int32, (RATES, LANES), 1)
    slope_q = RATES - 1 - RATES // 2 - lax.broadcasted_iota(jnp.int32, (RATES, LANES), 0)

    def at(q, row):
        return (q * rows + row) * chunks

    def left(value, amount):
        return value if amount % LANES == 0 else pltpu.roll(value, -amount % LANES, 1)

    for t in range(rows):
        base = t * ROW + HEAD + chunks
        inner = jnp.broadcast_to(e_ref[pl.ds(base - 1, 1), :], (RATES, LANES))
        outer = jnp.broadcast_to(e_ref[pl.ds(base, 1), :], (RATES, LANES))
        value = jnp.where(lane_q >= slope_q * t + LANES, inner, outer)
        value = left(value, (RATES - 1 - RATES // 2) * t)
        for part in (t // 2, t - t // 2):
            if part:
                value = pltpu.roll(value, 0, 1, stride=part, stride_axis=0)
        halo[0, t] = jnp.where(last, jnp.zeros_like(value), value)
    for level in range(depth - 1):
        m = 1 << level
        for r in range(rows // (2 * m)):
            for d in range(m):
                first = halo[level, 2 * r * m + d]
                second = halo[level, (2 * r + 1) * m + d]
                for odd in range(2):
                    halo[level + 1, r * 2 * m + 2 * d + odd] = first + left(second, d + odd)

    def windows(t):
        return [e_ref[pl.ds(t * ROW + HEAD + shift, chunks), :] for shift in (-1, 0, 1)]

    def shifted(seen, amount):
        down = 1 if amount >= 0 else 0
        lanes = amount % LANES
        if lanes == 0:
            return seen[down + (amount - lanes) // LANES + 1 - down]
        return left(jnp.where(lane >= lanes, seen[down], seen[down + 1]), lanes)

    for r in range(rows // 2):
        even, odd_row = windows(2 * r), windows(2 * r + 1)
        for q in range(RATES):
            slope = q - RATES // 2
            first = shifted(even, slope * 2 * r)
            second = shifted(odd_row, slope * (2 * r + 1))
            ahead = shifted(odd_row, slope * (2 * r + 1) + 1)
            ahead = jnp.where(edge, jnp.zeros_like(ahead), ahead)
            levels[1][pl.ds(at(q, 2 * r), chunks), :] = first + second
            levels[1][pl.ds(at(q, 2 * r + 1), chunks), :] = first + ahead

    def tree(step, carry):
        for level in range(1, depth):
            m = 1 << level
            source = levels[level]
            for r in range(rows // (2 * m)):
                for d in range(m):
                    for sub in range(UNROLL):
                        q = step * UNROLL + sub
                        row_b = (2 * r + 1) * m + d
                        where_b = pl.multiple_of(at(q, row_b), 8)
                        first = source[pl.ds(pl.multiple_of(at(q, 2 * r * m + d), 8), chunks), :]
                        second = source[pl.ds(where_b, chunks), :]
                        ahead = source[pl.ds(where_b + 1, chunks), :]
                        beyond = jnp.broadcast_to(halo[level, row_b, pl.ds(RATES - 1 - q, 1), :], (chunks, LANES))
                        ahead = jnp.where(final, beyond, ahead)
                        for odd in range(2):
                            k = d + odd
                            moved = second
                            if k:
                                moved = left(jnp.where(lane >= k, second, ahead), k)
                            row = r * 2 * m + 2 * d + odd
                            value = first + moved
                            if level + 1 < depth:
                                levels[level + 1][pl.ds(pl.multiple_of(at(q, row), 8), chunks), :] = value
                            else:
                                out[q, row * chunks : (row + 1) * chunks] = value
        for sub in range(UNROLL):
            q = step * UNROLL + sub
            pltpu.make_async_copy(out.at[q], out_hbm.at[q], out_sem.at[q]).start()
        return carry

    lax.fori_loop(0, RATES // UNROLL, tree, 0)
    for q in range(RATES):
        pltpu.make_async_copy(out.at[q], out_hbm.at[q], out_sem.at[q]).wait()


def on_device(channels, fines, spectra):
    rows, _, columns = spectra.shape
    chunks = columns // LANES
    depth = rows.bit_length() - 1
    assert (RATES // 2) * (rows - 1) <= LANES and rows == 1 << depth
    others = channels // 2 - 1
    half = rows // 2
    size = half // PIECES * chunks
    vmem = functools.partial(pltpu.VMEM, dtype=jnp.float32)
    dma = pltpu.SemaphoreType.DMA
    x = spectra.reshape(rows * chunks, LANES)
    normed = pl.pallas_call(
        functools.partial(comm_kernel, channels, fines, rows, chunks),
        out_shape=jax.ShapeDtypeStruct((rows * ROW, LANES), jnp.float32),
        in_specs=[pl.BlockSpec(memory_space=pltpu.VMEM)],
        out_specs=pl.BlockSpec(memory_space=pltpu.VMEM),
        scratch_shapes=[
            vmem((2, 2, half, LANES)), vmem((2, 2, half, LANES)),
            vmem((PIECES, size, LANES)), vmem((PIECES, size, LANES)),
            vmem((others, PIECES, size, LANES)), vmem((PIECES, size, LANES)), vmem((PIECES, size, LANES)),
            vmem((2, half, LANES)), vmem((2, half, LANES)), vmem((others, 2, half, LANES)),
            vmem((2, half, LANES)), vmem((2, half, LANES)),
            dma((2,)), dma((2,)), dma((PIECES + 2,)), dma((PIECES + 2,)),
            dma((others, PIECES + 1)), dma((others, PIECES + 1)), dma((PIECES + 1,)), dma((PIECES + 1,)),
        ],
        compiler_params=pltpu.CompilerParams(collective_id=0, has_side_effects=True, vmem_limit_bytes=8 << 20),
        name="normalize",
    )(x)
    stored = RATES * rows * chunks + 8
    out = pl.pallas_call(
        functools.partial(tree_kernel, channels, fines, rows, chunks),
        out_shape=jax.ShapeDtypeStruct((RATES, rows * chunks, LANES), jnp.float32),
        in_specs=[pl.BlockSpec(memory_space=pltpu.VMEM)],
        out_specs=pl.BlockSpec(memory_space=pl.ANY),
        scratch_shapes=[vmem((RATES, rows * chunks, LANES)), vmem((depth, rows, RATES, LANES))]
        + [vmem((stored, LANES))] * (depth - 1)
        + [dma((RATES,))],
        compiler_params=pltpu.CompilerParams(vmem_limit_bytes=20 << 20),
        name="tree",
    )(normed)
    return out.reshape(RATES, rows, 1, columns)


def solution(mesh):
    body = functools.partial(on_device, mesh.shape["coarse"], mesh.shape["fine"])
    in_specs = (P(None, ("band", "coarse"), "fine"),)
    out_specs = P(None, None, ("band", "coarse"), "fine")
    return jax.shard_map(body, mesh=mesh, in_specs=in_specs, out_specs=out_specs, check_vma=False)
```

```python
import functools

import jax
import jax.numpy as jnp
from jax import lax
from jax.experimental import pallas as pl
from jax.experimental.pallas import tpu as pltpu
from jax.sharding import PartitionSpec as P

RATES = 8
LANES = 128
PIECES = 4
UNROLL = 2
ROW = 18
HEAD = 1
MESH = pl.DeviceIdType.MESH


def comm_kernel(
    channels, fines, rows, chunks, x_hbm, e_ref,
    x_ref, edge, edge_a, edge_1, edge_b, edge_n, halo, part_a, sum_1, part_b, inv_1, part_c,
    x_sem, a_send, a_recv, b_send, b_recv, c_send, c_recv, h_send, h_recv, ready,
):
    half_rows = rows // 2
    piece_rows = half_rows // PIECES
    size = piece_rows * chunks
    others = channels // 2 - 1
    c = lax.axis_index("coarse")
    f = lax.axis_index("fine")
    mine = c % 2
    theirs = 1 - mine
    pair = c // 2
    next_c = (c + 1) % channels
    prev_c = (c + channels - 1) % channels
    partner = {"coarse": pair * 2 + theirs}
    peers = [{"coarse": ((pair + o) % (channels // 2)) * 2 + mine} for o in range(1, others + 1)]
    place = c * fines + f
    after = (place + 1) % (channels * fines)
    before = (place + channels * fines - 1) % (channels * fines)
    around = [
        {"coarse": after // fines, "fine": after % fines},
        {"coarse": before // fines, "fine": before % fines},
    ]

    def signal(sem, **device):
        pl.semaphore_signal(sem, inc=1, device_id=device, device_id_type=MESH)

    fetch = pltpu.make_async_copy(x_hbm, x_ref, x_sem)
    fetch.start()
    barrier = pltpu.get_barrier_semaphore()
    for o in range(1, channels):
        signal(barrier, coarse=(c + o) % channels)

    @pl.when(f > 0)
    def _():
        signal(barrier, fine=f - 1)

    @pl.when(f < fines - 1)
    def _():
        signal(barrier, fine=f + 1)

    inner = jnp.logical_and(f > 0, f < fines - 1).astype(jnp.int32)
    pl.semaphore_wait(barrier, channels + inner)

    @pl.when(f == 0)
    def _():
        signal(ready.at[0], fine=f + 1)

    @pl.when(f == fines - 1)
    def _():
        signal(ready.at[2], fine=f - 1)

    started = []

    def send(src, dst, send_sem, recv_sem, device):
        copy = pltpu.make_async_remote_copy(
            src_ref=src, dst_ref=dst, send_sem=send_sem, recv_sem=recv_sem,
            device_id=device, device_id_type=MESH,
        )
        copy.start()
        started.append(copy)
        return copy

    def piece_start(half, p):
        return pl.multiple_of((half * half_rows + p * piece_rows) * chunks, 8)

    fetch.wait()
    edge[0] = x_ref[pl.ds(chunks - 1, rows, stride=chunks), :]
    edge[1] = x_ref[pl.ds(0, rows, stride=chunks), :]
    a_copies = [
        send(x_ref.at[pl.ds(piece_start(theirs, p), size), :], part_a.at[p], a_send.at[p], a_recv.at[p], partner)
        for p in range(1)
    ]
    edge_copy = send(edge, edge_a, a_send.at[PIECES], a_recv.at[PIECES], partner)
    a_copies += [
        send(x_ref.at[pl.ds(piece_start(theirs, p), size), :], part_a.at[p], a_send.at[p], a_recv.at[p], partner)
        for p in range(1, PIECES)
    ]

    edge_copy.wait_recv()
    edge_1[...] = edge[...] + edge_a[...]
    edge_b_copies = [
        send(edge_1, edge_b.at[o], b_send.at[o, PIECES], b_recv.at[o, PIECES], peers[o])
        for o in range(others)
    ]
    b_copies = []
    for p in range(PIECES):
        a_copies[p].wait_recv()
        sum_1[p] = x_ref[pl.ds(piece_start(mine, p), size), :] + part_a[p]
        b_copies.append([
            send(sum_1.at[p], part_b.at[o, p], b_send.at[o, p], b_recv.at[o, p], peers[o])
            for o in range(others)
        ])

    @pl.when(f > 0)
    def _():
        pl.semaphore_wait(ready.at[0], 1)

    @pl.when(jnp.logical_and(f > 0, f < fines - 1))
    def _():
        signal(ready.at[0], fine=f + 1)

    @pl.when(f == fines - 1)
    def _():
        signal(ready.at[1], coarse=prev_c)

    @pl.when(f < fines - 1)
    def _():
        pl.semaphore_wait(ready.at[2], 1)

    @pl.when(jnp.logical_and(f > 0, f < fines - 1))
    def _():
        signal(ready.at[2], fine=f - 1)

    @pl.when(f == 0)
    def _():
        signal(ready.at[3], coarse=next_c)

    total = edge_1[...]
    for o in range(others):
        edge_b_copies[o].wait_recv()
        total = total + edge_b[o]
    edge_n[...] = edge[...] * (1.0 / (total / channels)) - 1.0

    @pl.when(f == fines - 1)
    def _():
        pl.semaphore_wait(ready.at[1], 1)

    @pl.when(f == 0)
    def _():
        pl.semaphore_wait(ready.at[3], 1)

    halo_copies = [
        send(edge_n.at[side], halo.at[side], h_send.at[side], h_recv.at[side], around[side])
        for side in range(2)
    ]

    def put(half, p, inverse):
        normed = x_ref[pl.ds(piece_start(half, p), size), :] * inverse - 1.0
        for i in range(piece_rows):
            t = half * half_rows + p * piece_rows + i
            e_ref[pl.ds(t * ROW + HEAD, chunks), :] = normed[i * chunks : (i + 1) * chunks]

    c_copies = []
    for p in range(PIECES):
        total = sum_1[p]
        for o in range(others):
            b_copies[p][o].wait_recv()
            total = total + part_b[o, p]
        inv_1[p] = 1.0 / (total / channels)
        c_copies.append(send(inv_1.at[p], part_c.at[p], c_send.at[p], c_recv.at[p], partner))
        put(mine, p, inv_1[p])
    for p in range(PIECES):
        c_copies[p].wait_recv()
        put(theirs, p, part_c[p])

    at_end = [place == 0, place == channels * fines - 1]
    at_row = [HEAD - 1, HEAD + chunks]
    for side in range(2):
        halo_copies[side].wait_recv()
        normed = jnp.where(at_end[side], jnp.zeros((rows, LANES), jnp.float32), halo[side])
        for t in range(rows):
            e_ref[pl.ds(t * ROW + at_row[side], 1), :] = normed[t : t + 1]
    for copy in started:
        copy.wait_send()


def tree_kernel(channels, fines, rows, chunks, e_ref, out_hbm, out, halo, *rest):
    levels = (None,) + rest[:-1]
    out_sem = rest[-1]
    depth = len(levels)
    last = jnp.logical_and(
        lax.axis_index("coarse") == channels - 1, lax.axis_index("fine") == fines - 1
    )
    lane = lax.broadcasted_iota(jnp.int32, (chunks, LANES), 1)
    chunk = lax.broadcasted_iota(jnp.int32, (chunks, LANES), 0)
    final = chunk == chunks - 1
    edge = jnp.logical_and(jnp.logical_and(final, lane == LANES - 1), last)
    lane_q = lax.broadcasted_iota(jnp.int32, (RATES, LANES), 1)
    slope_q = RATES - 1 - RATES // 2 - lax.broadcasted_iota(jnp.int32, (RATES, LANES), 0)

    def at(q, row):
        return (q * rows + row) * chunks

    def left(value, amount):
        return value if amount % LANES == 0 else pltpu.roll(value, -amount % LANES, 1)

    for t in range(rows):
        base = t * ROW + HEAD + chunks
        inner = jnp.broadcast_to(e_ref[pl.ds(base - 1, 1), :], (RATES, LANES))
        outer = jnp.broadcast_to(e_ref[pl.ds(base, 1), :], (RATES, LANES))
        value = jnp.where(lane_q >= slope_q * t + LANES, inner, outer)
        value = left(value, (RATES - 1 - RATES // 2) * t)
        for part in (t // 2, t - t // 2):
            if part:
                value = pltpu.roll(value, 0, 1, stride=part, stride_axis=0)
        halo[0, t] = jnp.where(last, jnp.zeros_like(value), value)
    for level in range(depth - 1):
        m = 1 << level
        for r in range(rows // (2 * m)):
            for d in range(m):
                first = halo[level, 2 * r * m + d]
                second = halo[level, (2 * r + 1) * m + d]
                for odd in range(2):
                    halo[level + 1, r * 2 * m + 2 * d + odd] = first + left(second, d + odd)

    def windows(t):
        return [e_ref[pl.ds(t * ROW + HEAD + shift, chunks), :] for shift in (-1, 0, 1)]

    def shifted(seen, amount):
        down = 1 if amount >= 0 else 0
        lanes = amount % LANES
        if lanes == 0:
            return seen[down + (amount - lanes) // LANES + 1 - down]
        return left(jnp.where(lane >= lanes, seen[down], seen[down + 1]), lanes)

    for r in range(rows // 2):
        even, odd_row = windows(2 * r), windows(2 * r + 1)
        for q in range(RATES):
            slope = q - RATES // 2
            first = shifted(even, slope * 2 * r)
            second = shifted(odd_row, slope * (2 * r + 1))
            ahead = shifted(odd_row, slope * (2 * r + 1) + 1)
            ahead = jnp.where(edge, jnp.zeros_like(ahead), ahead)
            levels[1][pl.ds(at(q, 2 * r), chunks), :] = first + second
            levels[1][pl.ds(at(q, 2 * r + 1), chunks), :] = first + ahead

    def tree(step, carry):
        for level in range(1, depth):
            m = 1 << level
            source = levels[level]
            for r in range(rows // (2 * m)):
                for d in range(m):
                    for sub in range(UNROLL):
                        q = step * UNROLL + sub
                        row_b = (2 * r + 1) * m + d
                        where_b = pl.multiple_of(at(q, row_b), 8)
                        first = source[pl.ds(pl.multiple_of(at(q, 2 * r * m + d), 8), chunks), :]
                        second = source[pl.ds(where_b, chunks), :]
                        ahead = source[pl.ds(where_b + 1, chunks), :]
                        beyond = jnp.broadcast_to(halo[level, row_b, pl.ds(RATES - 1 - q, 1), :], (chunks, LANES))
                        ahead = jnp.where(final, beyond, ahead)
                        for odd in range(2):
                            k = d + odd
                            moved = second
                            if k:
                                moved = left(jnp.where(lane >= k, second, ahead), k)
                            row = r * 2 * m + 2 * d + odd
                            value = first + moved
                            if level + 1 < depth:
                                levels[level + 1][pl.ds(pl.multiple_of(at(q, row), 8), chunks), :] = value
                            else:
                                out[q, row * chunks : (row + 1) * chunks] = value
        for sub in range(UNROLL):
            q = step * UNROLL + sub
            pltpu.make_async_copy(out.at[q], out_hbm.at[q], out_sem.at[q]).start()
        return carry

    lax.fori_loop(0, RATES // UNROLL, tree, 0)
    for q in range(RATES):
        pltpu.make_async_copy(out.at[q], out_hbm.at[q], out_sem.at[q]).wait()


def on_device(channels, fines, spectra):
    rows, _, columns = spectra.shape
    chunks = columns // LANES
    depth = rows.bit_length() - 1
    assert (RATES // 2) * (rows - 1) <= LANES and rows == 1 << depth
    others = channels // 2 - 1
    half = rows // 2
    size = half // PIECES * chunks
    vmem = functools.partial(pltpu.VMEM, dtype=jnp.float32)
    dma = pltpu.SemaphoreType.DMA
    x = pltpu.with_memory_space_constraint(spectra.reshape(rows * chunks, LANES), pltpu.HBM)
    normed = pl.pallas_call(
        functools.partial(comm_kernel, channels, fines, rows, chunks),
        out_shape=jax.ShapeDtypeStruct((rows * ROW, LANES), jnp.float32),
        in_specs=[pl.BlockSpec(memory_space=pltpu.HBM)],
        out_specs=pl.BlockSpec(memory_space=pltpu.VMEM),
        scratch_shapes=[
            vmem((rows * chunks, LANES)),
            vmem((2, rows, LANES)), vmem((2, rows, LANES)), vmem((2, rows, LANES)),
            vmem((others, 2, rows, LANES)), vmem((2, rows, LANES)), vmem((2, rows, LANES)),
            vmem((PIECES, size, LANES)), vmem((PIECES, size, LANES)),
            vmem((others, PIECES, size, LANES)), vmem((PIECES, size, LANES)), vmem((PIECES, size, LANES)),
            dma, dma((PIECES + 1,)), dma((PIECES + 1,)),
            dma((others, PIECES + 1)), dma((others, PIECES + 1)), dma((PIECES,)), dma((PIECES,)),
            dma((2,)), dma((2,)), pltpu.SemaphoreType.REGULAR((4,)),
        ],
        compiler_params=pltpu.CompilerParams(collective_id=0, has_side_effects=True, vmem_limit_bytes=8 << 20),
        name="normalize",
    )(x)
    stored = RATES * rows * chunks + 8
    out = pl.pallas_call(
        functools.partial(tree_kernel, channels, fines, rows, chunks),
        out_shape=jax.ShapeDtypeStruct((RATES, rows * chunks, LANES), jnp.float32),
        in_specs=[pl.BlockSpec(memory_space=pltpu.VMEM)],
        out_specs=pl.BlockSpec(memory_space=pl.ANY),
        scratch_shapes=[vmem((RATES, rows * chunks, LANES)), vmem((depth, rows, RATES, LANES))]
        + [vmem((stored, LANES))] * (depth - 1)
        + [dma((RATES,))],
        compiler_params=pltpu.CompilerParams(vmem_limit_bytes=20 << 20),
        name="tree",
    )(normed)
    return out.reshape(RATES, rows, 1, columns)


def solution(mesh):
    body = functools.partial(on_device, mesh.shape["coarse"], mesh.shape["fine"])
    in_specs = (P(None, ("band", "coarse"), "fine"),)
    out_specs = P(None, None, ("band", "coarse"), "fine")
    return jax.shard_map(body, mesh=mesh, in_specs=in_specs, out_specs=out_specs, check_vma=False)
```

```python
import functools

import jax
import jax.numpy as jnp
from jax import lax
from jax.experimental import pallas as pl
from jax.experimental.pallas import tpu as pltpu
from jax.sharding import PartitionSpec as P

RATES = 8
LANES = 128
PIECES = 4
UNROLL = 2
ROW = 18
HEAD = 1
MESH = pl.DeviceIdType.MESH


def comm_kernel(
    channels, fines, rows, chunks, x_hbm, e_ref,
    x_ref, edge, edge_a, edge_1, edge_b, edge_n, halo, part_a, sum_1, part_b, inv_1, part_c,
    x_sem, a_send, a_recv, b_send, b_recv, c_send, c_recv, h_send, h_recv, ready,
):
    half_rows = rows // 2
    piece_rows = half_rows // PIECES
    size = piece_rows * chunks
    others = channels // 2 - 1
    c = lax.axis_index("coarse")
    f = lax.axis_index("fine")
    mine = c % 2
    theirs = 1 - mine
    pair = c // 2
    next_c = (c + 1) % channels
    prev_c = (c + channels - 1) % channels
    partner = {"coarse": pair * 2 + theirs}
    peers = [{"coarse": ((pair + o) % (channels // 2)) * 2 + mine} for o in range(1, others + 1)]
    place = c * fines + f
    after = (place + 1) % (channels * fines)
    before = (place + channels * fines - 1) % (channels * fines)
    around = [
        {"coarse": after // fines, "fine": after % fines},
        {"coarse": before // fines, "fine": before % fines},
    ]

    def signal(sem, **device):
        pl.semaphore_signal(sem, inc=1, device_id=device, device_id_type=MESH)

    fetch = pltpu.make_async_copy(x_hbm, x_ref, x_sem)
    fetch.start()
    barrier = pltpu.get_barrier_semaphore()
    for o in range(1, channels):
        signal(barrier, coarse=(c + o) % channels)

    @pl.when(f > 0)
    def _():
        signal(barrier, fine=f - 1)

    @pl.when(f < fines - 1)
    def _():
        signal(barrier, fine=f + 1)

    inner = jnp.logical_and(f > 0, f < fines - 1).astype(jnp.int32)
    pl.semaphore_wait(barrier, channels + inner)

    @pl.when(f == 0)
    def _():
        signal(ready.at[0], fine=f + 1)

    @pl.when(f == fines - 1)
    def _():
        signal(ready.at[2], fine=f - 1)

    started = []

    def send(src, dst, send_sem, recv_sem, device):
        copy = pltpu.make_async_remote_copy(
            src_ref=src, dst_ref=dst, send_sem=send_sem, recv_sem=recv_sem,
            device_id=device, device_id_type=MESH,
        )
        copy.start()
        started.append(copy)
        return copy

    def piece_start(half, p):
        return pl.multiple_of((half * half_rows + p * piece_rows) * chunks, 8)

    fetch.wait()
    edge[0] = x_ref[pl.ds(chunks - 1, rows, stride=chunks), :]
    edge[1] = x_ref[pl.ds(0, rows, stride=chunks), :]
    edge_copy = send(edge, edge_a, a_send.at[PIECES], a_recv.at[PIECES], partner)
    a_copies = [
        send(x_ref.at[pl.ds(piece_start(theirs, p), size), :], part_a.at[p], a_send.at[p], a_recv.at[p], partner)
        for p in range(PIECES)
    ]
    edge_copy.wait_recv()
    edge_1[...] = edge[...] + edge_a[...]
    edge_b_copies = [
        send(edge_1, edge_b.at[o], b_send.at[o, PIECES], b_recv.at[o, PIECES], peers[o])
        for o in range(others)
    ]
    b_copies = []
    for p in range(PIECES):
        a_copies[p].wait_recv()
        sum_1[p] = x_ref[pl.ds(piece_start(mine, p), size), :] + part_a[p]
        b_copies.append([
            send(sum_1.at[p], part_b.at[o, p], b_send.at[o, p], b_recv.at[o, p], peers[o])
            for o in range(others)
        ])

    @pl.when(f > 0)
    def _():
        pl.semaphore_wait(ready.at[0], 1)

    @pl.when(jnp.logical_and(f > 0, f < fines - 1))
    def _():
        signal(ready.at[0], fine=f + 1)

    @pl.when(f == fines - 1)
    def _():
        signal(ready.at[1], coarse=prev_c)

    @pl.when(f < fines - 1)
    def _():
        pl.semaphore_wait(ready.at[2], 1)

    @pl.when(jnp.logical_and(f > 0, f < fines - 1))
    def _():
        signal(ready.at[2], fine=f - 1)

    @pl.when(f == 0)
    def _():
        signal(ready.at[3], coarse=next_c)

    total = edge_1[...]
    for o in range(others):
        edge_b_copies[o].wait_recv()
        total = total + edge_b[o]
    edge_n[...] = edge[...] * (1.0 / (total / channels)) - 1.0

    @pl.when(f == fines - 1)
    def _():
        pl.semaphore_wait(ready.at[1], 1)

    @pl.when(f == 0)
    def _():
        pl.semaphore_wait(ready.at[3], 1)

    halo_copies = [
        send(edge_n.at[side], halo.at[side], h_send.at[side], h_recv.at[side], around[side])
        for side in range(2)
    ]

    def put(half, p, inverse):
        normed = x_ref[pl.ds(piece_start(half, p), size), :] * inverse - 1.0
        for i in range(piece_rows):
            t = half * half_rows + p * piece_rows + i
            e_ref[pl.ds(t * ROW + HEAD, chunks), :] = normed[i * chunks : (i + 1) * chunks]

    c_copies = []
    for p in range(PIECES):
        total = sum_1[p]
        for o in range(others):
            b_copies[p][o].wait_recv()
            total = total + part_b[o, p]
        inv_1[p] = 1.0 / (total / channels)
        c_copies.append(send(inv_1.at[p], part_c.at[p], c_send.at[p], c_recv.at[p], partner))
    for p in range(PIECES):
        put(mine, p, inv_1[p])
    at_end = [place == 0, place == channels * fines - 1]
    at_row = [HEAD - 1, HEAD + chunks]
    for side in range(2):
        halo_copies[side].wait_recv()
        normed = jnp.where(at_end[side], jnp.zeros((rows, LANES), jnp.float32), halo[side])
        for t in range(rows):
            e_ref[pl.ds(t * ROW + at_row[side], 1), :] = normed[t : t + 1]
    for p in range(PIECES):
        c_copies[p].wait_recv()
        put(theirs, p, part_c[p])

    for copy in started:
        copy.wait_send()


def tree_kernel(channels, fines, rows, chunks, e_ref, out_hbm, out, halo, *rest):
    levels = (None,) + rest[:-1]
    out_sem = rest[-1]
    depth = len(levels)
    last = jnp.logical_and(
        lax.axis_index("coarse") == channels - 1, lax.axis_index("fine") == fines - 1
    )
    lane = lax.broadcasted_iota(jnp.int32, (chunks, LANES), 1)
    chunk = lax.broadcasted_iota(jnp.int32, (chunks, LANES), 0)
    final = chunk == chunks - 1
    edge = jnp.logical_and(jnp.logical_and(final, lane == LANES - 1), last)
    lane_q = lax.broadcasted_iota(jnp.int32, (RATES, LANES), 1)
    slope_q = RATES - 1 - RATES // 2 - lax.broadcasted_iota(jnp.int32, (RATES, LANES), 0)

    def at(q, row):
        return (q * rows + row) * chunks

    def left(value, amount):
        return value if amount % LANES == 0 else pltpu.roll(value, -amount % LANES, 1)

    for t in range(rows):
        base = t * ROW + HEAD + chunks
        inner = jnp.broadcast_to(e_ref[pl.ds(base - 1, 1), :], (RATES, LANES))
        outer = jnp.broadcast_to(e_ref[pl.ds(base, 1), :], (RATES, LANES))
        value = jnp.where(lane_q >= slope_q * t + LANES, inner, outer)
        value = left(value, (RATES - 1 - RATES // 2) * t)
        for part in (t // 2, t - t // 2):
            if part:
                value = pltpu.roll(value, 0, 1, stride=part, stride_axis=0)
        halo[0, t] = jnp.where(last, jnp.zeros_like(value), value)
    for level in range(depth - 1):
        m = 1 << level
        for r in range(rows // (2 * m)):
            for d in range(m):
                first = halo[level, 2 * r * m + d]
                second = halo[level, (2 * r + 1) * m + d]
                for odd in range(2):
                    halo[level + 1, r * 2 * m + 2 * d + odd] = first + left(second, d + odd)

    def windows(t):
        return [e_ref[pl.ds(t * ROW + HEAD + shift, chunks), :] for shift in (-1, 0, 1)]

    def shifted(seen, amount):
        down = 1 if amount >= 0 else 0
        lanes = amount % LANES
        if lanes == 0:
            return seen[down + (amount - lanes) // LANES + 1 - down]
        return left(jnp.where(lane >= lanes, seen[down], seen[down + 1]), lanes)

    for r in range(rows // 2):
        even, odd_row = windows(2 * r), windows(2 * r + 1)
        for q in range(RATES):
            slope = q - RATES // 2
            first = shifted(even, slope * 2 * r)
            second = shifted(odd_row, slope * (2 * r + 1))
            ahead = shifted(odd_row, slope * (2 * r + 1) + 1)
            ahead = jnp.where(edge, jnp.zeros_like(ahead), ahead)
            levels[1][pl.ds(at(q, 2 * r), chunks), :] = first + second
            levels[1][pl.ds(at(q, 2 * r + 1), chunks), :] = first + ahead

    def tree(step, carry):
        for level in range(1, depth):
            m = 1 << level
            source = levels[level]
            for r in range(rows // (2 * m)):
                for d in range(m):
                    for sub in range(UNROLL):
                        q = step * UNROLL + sub
                        row_b = (2 * r + 1) * m + d
                        where_b = pl.multiple_of(at(q, row_b), 8)
                        first = source[pl.ds(pl.multiple_of(at(q, 2 * r * m + d), 8), chunks), :]
                        second = source[pl.ds(where_b, chunks), :]
                        ahead = source[pl.ds(where_b + 1, chunks), :]
                        beyond = jnp.broadcast_to(halo[level, row_b, pl.ds(RATES - 1 - q, 1), :], (chunks, LANES))
                        ahead = jnp.where(final, beyond, ahead)
                        for odd in range(2):
                            k = d + odd
                            moved = second
                            if k:
                                moved = left(jnp.where(lane >= k, second, ahead), k)
                            row = r * 2 * m + 2 * d + odd
                            value = first + moved
                            if level + 1 < depth:
                                levels[level + 1][pl.ds(pl.multiple_of(at(q, row), 8), chunks), :] = value
                            else:
                                out[q, row * chunks : (row + 1) * chunks] = value
        for sub in range(UNROLL):
            q = step * UNROLL + sub
            pltpu.make_async_copy(out.at[q], out_hbm.at[q], out_sem.at[q]).start()
        return carry

    lax.fori_loop(0, RATES // UNROLL, tree, 0)
    for q in range(RATES):
        pltpu.make_async_copy(out.at[q], out_hbm.at[q], out_sem.at[q]).wait()


def on_device(channels, fines, spectra):
    rows, _, columns = spectra.shape
    chunks = columns // LANES
    depth = rows.bit_length() - 1
    assert (RATES // 2) * (rows - 1) <= LANES and rows == 1 << depth
    others = channels // 2 - 1
    half = rows // 2
    size = half // PIECES * chunks
    vmem = functools.partial(pltpu.VMEM, dtype=jnp.float32)
    dma = pltpu.SemaphoreType.DMA
    x = pltpu.with_memory_space_constraint(spectra.reshape(rows * chunks, LANES), pltpu.HBM)
    normed = pl.pallas_call(
        functools.partial(comm_kernel, channels, fines, rows, chunks),
        out_shape=jax.ShapeDtypeStruct((rows * ROW, LANES), jnp.float32),
        in_specs=[pl.BlockSpec(memory_space=pltpu.HBM)],
        out_specs=pl.BlockSpec(memory_space=pltpu.VMEM),
        scratch_shapes=[
            vmem((rows * chunks, LANES)),
            vmem((2, rows, LANES)), vmem((2, rows, LANES)), vmem((2, rows, LANES)),
            vmem((others, 2, rows, LANES)), vmem((2, rows, LANES)), vmem((2, rows, LANES)),
            vmem((PIECES, size, LANES)), vmem((PIECES, size, LANES)),
            vmem((others, PIECES, size, LANES)), vmem((PIECES, size, LANES)), vmem((PIECES, size, LANES)),
            dma, dma((PIECES + 1,)), dma((PIECES + 1,)),
            dma((others, PIECES + 1)), dma((others, PIECES + 1)), dma((PIECES,)), dma((PIECES,)),
            dma((2,)), dma((2,)), pltpu.SemaphoreType.REGULAR((4,)),
        ],
        compiler_params=pltpu.CompilerParams(collective_id=0, has_side_effects=True, vmem_limit_bytes=8 << 20),
        name="normalize",
    )(x)
    stored = RATES * rows * chunks + 8
    out = pl.pallas_call(
        functools.partial(tree_kernel, channels, fines, rows, chunks),
        out_shape=jax.ShapeDtypeStruct((RATES, rows * chunks, LANES), jnp.float32),
        in_specs=[pl.BlockSpec(memory_space=pltpu.VMEM)],
        out_specs=pl.BlockSpec(memory_space=pl.ANY),
        scratch_shapes=[vmem((RATES, rows * chunks, LANES)), vmem((depth, rows, RATES, LANES))]
        + [vmem((stored, LANES))] * (depth - 1)
        + [dma((RATES,))],
        compiler_params=pltpu.CompilerParams(vmem_limit_bytes=20 << 20),
        name="tree",
    )(normed)
    return out.reshape(RATES, rows, 1, columns)


def solution(mesh):
    body = functools.partial(on_device, mesh.shape["coarse"], mesh.shape["fine"])
    in_specs = (P(None, ("band", "coarse"), "fine"),)
    out_specs = P(None, None, ("band", "coarse"), "fine")
    return jax.shard_map(body, mesh=mesh, in_specs=in_specs, out_specs=out_specs, check_vma=False)
```
